256 devices in a mesh: aux: 32 (over y, x, core), vir: 8 (over z).
Axes of the slice: x: 4, y: 4, z: 8, core: 2. Of those that a mesh axis runs over, the one named last changes fastest.
Arguments:
- integrals: float32 [4096, 128, 1024], P('aux', None, 'vir'), may hold values from -0.024964112 to 0.024964112, as said below
- occupied_energy: float32 [128], P('aux'), may hold values from -3.5 to -2
- virtual_energy: float32 [1024], P('vir'), may hold values from 1.5 to 6
- right_side: float32 [1024, 128], P('vir', 'aux'), may hold values from -500 to 500
Outputs:
- solution: float32 [1024, 128], P('vir', 'aux')
- residual: float32 [1024, 128], P('vir', 'aux')
The draws below stay inside these ranges and needn't reach their ends.
Inputs may be any that keep to these rules, and one draw needn't show every extreme that they name: Entries of the integrals are of order one over the fourth root of 536870912.
All inputs are finite; a program needn't handle non-finite values.
Results may differ from the reference program's by a relative error of at most 0.0003.
Values sent between devices are 32-bit elements; how exact they have to be, the bound alone decides.
A program may use at most 128 MiB of HBM per device.

```python
import jax
import jax.numpy as jnp
from jax import lax

O = 128
V = 1024
P_SIZE = 4096
ITERS = 3


def draw_integrals(key, part):
    factor = 0.4 ** 0.5 * float(P_SIZE * O * V) ** (-0.25)
    values = jax.random.truncated_normal(key, -3.7, 3.7, (P_SIZE, O, V), jnp.float32)
    return values * factor


def draw_right_side(key, part):
    key_base = jax.random.fold_in(key, 11)
    key_rows = jax.random.fold_in(key, 12)
    key_cols = jax.random.fold_in(key, 13)
    row_scale = 3.0 ** (jnp.arange(V, dtype=jnp.float32) / V) * jnp.exp(jax.random.uniform(key_rows, (V,), jnp.float32, 0.0, 1.2))
    col_scale = 3.0 ** (jnp.arange(O, dtype=jnp.float32) / O) * jnp.exp(jax.random.uniform(key_cols, (O,), jnp.float32, 0.0, 1.2))
    fluctuation = jax.random.truncated_normal(key_base, -5.0, 5.0, (V, O), jnp.float32)
    return fluctuation * row_scale[:, None] * col_scale[None, :]


def level_of(stream_key, shape, pieces, smallest, high):
    def one(axis_at, blocks):
        heights = jax.random.uniform(jax.random.fold_in(jax.random.fold_in(stream_key, 6), axis_at), (blocks,), jnp.float32, smallest / len(pieces), high / len(pieces))
        return jnp.repeat(jnp.exp(heights), shape[axis_at] // blocks).reshape((-1,) + (1,) * (len(shape) - axis_at - 1))

    loudness = one(*pieces[0])
    for cut in pieces[1:]:
        loudness = loudness * one(*cut)
    return loudness


def setup_inputs(seed: int = 0) -> dict:
    splits = jax.random.split(jax.random.key(seed), 5)
    return {
        "integrals": draw_integrals(jax.random.fold_in(splits[4], 71), 0),
        "occupied_energy": jnp.clip(-3.5 + 1.5 * jax.random.uniform(splits[1], (O,), jnp.float32) ** level_of(splits[1], (O,), ((0, 32),), -0.2, 0.2), -3.5, -2.0),
        "virtual_energy": jnp.clip(1.5 + 4.5 * jax.random.uniform(splits[2], (V,), jnp.float32) ** level_of(splits[2], (V,), ((0, 8),), -0.2, 0.2), 1.5, 6.0),
        "right_side": draw_right_side(jax.random.fold_in(splits[4], 71), 0),
    }


HIGHEST = lax.Precision.HIGHEST


def apply_hessian(trial, integrals, energy_gap):
    def block(accumulated, block_ints):
        coulomb = jnp.einsum("pia,ai->p", block_ints, trial, precision=HIGHEST)
        coulomb_term = jnp.einsum("pia,p->ai", block_ints, coulomb, precision=HIGHEST)
        inter = jnp.einsum("pib,bj->pij", block_ints, trial, precision=HIGHEST)
        exchange_term = jnp.einsum("pij,pja->ai", inter, block_ints, precision=HIGHEST)
        return accumulated + 4.0 * coulomb_term - exchange_term, None

    blocks = integrals.reshape(P_SIZE // 128, 128, O, V)
    start = jnp.zeros((V, O), jnp.float32)
    accumulated, _ = lax.scan(block, start, blocks)
    return energy_gap * trial + accumulated


def reference(integrals, occupied_energy, virtual_energy, right_side):
    energy_gap = virtual_energy[:, None] - occupied_energy[None, :]
    solution = jnp.zeros_like(right_side)
    residual = right_side
    direction = right_side
    norm_now = jnp.sum(residual * residual)
    for step in range(ITERS):
        image = apply_hessian(direction, integrals, energy_gap)
        step_len = norm_now / jnp.sum(direction * image)
        solution = solution + step_len * direction
        residual = residual - step_len * image
        norm_next = jnp.sum(residual * residual)
        direction = residual + (norm_next / norm_now) * direction
        norm_now = norm_next
    return solution, residual
```

```python
import functools

import jax
import jax.numpy as jnp
from jax import lax
from jax.experimental import pallas as pl
from jax.experimental.pallas import tpu as pltpu
from jax.sharding import PartitionSpec as P

ITERS = 3
NZ = 8
NM = 16
NP = 16
O = 128
V = 1024
W = V + 128
MESH = pl.DeviceIdType.MESH
F32 = jnp.float32
BF16 = jnp.bfloat16
ARRIVAL = (4, 3, 5, 2, 6, 1, 7)


def total(x):
    return jnp.sum(jnp.sum(x, axis=0, keepdims=True), axis=1, keepdims=True)


def split(x):
    high = x.astype(BF16)
    return high, (x - high.astype(F32)).astype(BF16)


def kernel(
    ints, occ, vir, rhs, sol, res,
    recv, bhi, blo, d, r, img, part, cbuf, xbuf, zsend, zbuf, g, g2, gap, x, d2, zs, rr, fin,
    a2a_s, a2a_r, loc, iz_s, iz_r, ic, agz_s, agz_r, agx_s, agx_r, agc_s, agc_r,
    rsc, rsx_s, rsx_r, rsz_s, rsz_r, fs,
):
    a = lax.axis_index("aux")
    z = lax.axis_index("vir")
    c = lax.rem(a, 2)
    m = lax.div(a, 2)
    owner = lax.div(m, 8) == c
    partner = (2 * m + 1 - c, z)

    def at_z(k):
        return (a, lax.rem(z + k + NZ, NZ))

    def at_m(chip):
        return (2 * chip + c, z)

    def remote(src, dst, send, recv_sem, dev):
        return pltpu.make_async_remote_copy(
            src_ref=src, dst_ref=dst, send_sem=send, recv_sem=recv_sem, device_id=dev, device_id_type=MESH
        )

    def rows(ref, chip, count=8):
        return ref.at[pl.ds(pl.multiple_of(8 * chip, 8), count)]

    barrier = pltpu.get_barrier_semaphore()
    pl.semaphore_signal(barrier, inc=1, device_id=partner, device_id_type=MESH)
    for k in range(1, NZ):
        pl.semaphore_signal(barrier, inc=1, device_id=at_z(k), device_id_type=MESH)
    for j in range(1, NM):
        pl.semaphore_signal(barrier, inc=1, device_id=at_m(lax.rem(m + j, NM)), device_id_type=MESH)

    row = lax.broadcasted_iota(jnp.int32, (8, 128), 0)
    mine = lax.div(row, 4) == c
    occ_rows = jnp.zeros((8, 128), F32)
    for i in range(4):
        occ_rows = jnp.where(lax.rem(row, 4) == i, occ[i], occ_rows)
    own = rhs[...]
    g[:, 0:128] = jnp.where(mine, jnp.concatenate([own, own], axis=0), 0.0)
    g[:, V:W] = jnp.where(mine, jnp.broadcast_to(vir[...], (8, 128)) - occ_rows, 0.0)

    pl.semaphore_wait(barrier, 1 + NZ - 1 + NM - 1)

    def init_z(k):
        return remote(g.at[:, 0:128], g.at[:, k * 128:(k + 1) * 128], iz_s.at[k], iz_r.at[k], at_z(k))

    def exchange(k):
        to = lax.rem(z + k, NZ)
        return remote(ints.at[pl.ds(to * NP, NP)], recv.at[k], a2a_s.at[k], a2a_r.at[k], (a, to))

    for k in range(1, NZ):
        init_z(k).start()
    for k in ARRIVAL:
        exchange(k).start()
    local = pltpu.make_async_copy(ints.at[pl.ds(z * NP, NP)], recv.at[0], loc)
    local.start()

    def spread():
        def to_chip(j):
            return remote(
                rows(img, m), rows(img, m), agx_s.at[j], agx_r.at[lax.rem(m, 8)], at_m(lax.rem(m + j, NM))
            )

        def to_partner(t):
            block = rows(img, 8 * c + t)
            return remote(block, block, agc_s.at[t], agc_r.at[t], partner)

        def from_partner(t):
            block = rows(img, 8 * (1 - c) + t)
            return remote(block, block, agc_s.at[t], agc_r.at[t], partner)

        @pl.when(owner)
        def _():
            for j in range(1, NM):
                to_chip(j).start()
            to_partner(lax.rem(m, 8)).start()

        for t in range(8):
            @pl.when(8 * c + t != m)
            def _():
                block = rows(img, 8 * c + t)
                remote(block, block, agx_s.at[0], agx_r.at[t], partner).wait_recv()
                to_partner(t).start()

        for t in range(8):
            from_partner(t).wait_recv()
        for t in range(8):
            to_partner(t).wait_send()

        @pl.when(owner)
        def _():
            for j in range(1, NM):
                to_chip(j).wait_send()

    for k in range(1, NZ):
        init_z(k).wait_recv()
    swap = remote(g, g2, ic.at[0], ic.at[1], partner)
    swap.start()
    swap.wait_recv()
    gap[...] = g[:, V:W] + g2[:, V:W]

    @pl.when(owner)
    def _():
        rows(img, m)[...] = g[:, 0:V] + g2[:, 0:V]

    spread()
    swap.wait_send()
    for k in range(1, NZ):
        init_z(k).wait_send()

    first = img[...]
    d[...] = first
    r[...] = first
    rr[...] = jnp.broadcast_to(total(first * first), (8, 128))
    x[...] = jnp.zeros((8, 128), F32)

    def convert(k):
        def body(p, carry):
            high, low = split(recv[k, p])
            at = pl.ds(pl.multiple_of(p * 128, 128), 128)
            bhi[at, k * 128:(k + 1) * 128] = high
            blo[at, k * 128:(k + 1) * 128] = low
            return carry

        lax.fori_loop(0, NP, body, 0)

    local.wait()
    convert(0)
    for k in ARRIVAL:
        exchange(k).wait_recv()
        convert(k)

    def apply_local():
        high, low = split(d[...])
        d2[0:128, :] = high
        d2[128:256, :] = low
        eye = lax.broadcasted_iota(jnp.int32, (128, 128), 0) == lax.broadcasted_iota(jnp.int32, (128, 128), 1)
        contract = (((1,), (1,)), ((), ()))

        def inter(n, carry):
            at = pl.ds(pl.multiple_of(n * 512, 512), 512)
            both = lax.dot_general(bhi[at, :], d2[...], contract, preferred_element_type=F32)
            rest = lax.dot_general(blo[at, :], d2[0:128, :], contract, preferred_element_type=F32)
            y = both[:, 0:128] + both[:, 128:256] + rest
            for q in range(4):
                block = y[q * 128:(q + 1) * 128, :]
                coulomb = total(jnp.where(eye, block, 0.0))
                zh, zl = split(jnp.where(eye, 4.0 * coulomb, 0.0) - block)
                cols = pl.ds(pl.multiple_of(n * 512 + q * 128, 128), 128)
                zs[0:128, cols] = zh
                zs[128:256, cols] = zl
            return carry

        lax.fori_loop(0, NP // 4, inter, 0)

        def outer(n, carry):
            cols = pl.ds(pl.multiple_of(n * 256, 256), 256)
            both = jnp.dot(zs[...], bhi[:, cols], preferred_element_type=F32)
            rest = jnp.dot(zs[0:128, :], blo[:, cols], preferred_element_type=F32)
            part[:, cols] = both[0:128] + both[128:256] + rest
            return carry

        lax.fori_loop(0, V // 256, outer, 0)

    def reduce(width, tail):
        theirs = rows(part, 8 * (1 - c), 64).at[:, 0:width]
        pair = remote(theirs, cbuf.at[:, 0:width], rsc.at[0], rsc.at[1], partner)
        pair.start()
        pair.wait_recv()
        half = rows(part, 8 * c, 64)
        half[:, 0:width] = half[:, 0:width] + cbuf[:, 0:width]

        def to_chip(t):
            chip = 8 * c + t
            j = lax.rem(chip - m + NM, NM)
            return remote(
                rows(part, chip).at[:, 0:width], xbuf.at[j, :, 0:width], rsx_s.at[t], rsx_r.at[j], at_m(chip)
            )

        for t in range(8):
            @pl.when(8 * c + t != m)
            def _():
                to_chip(t).start()

        @pl.when(owner)
        def _():
            acc = rows(part, m)[:, 0:width]
            for j in range(1, NM):
                slot = xbuf.at[j, :, 0:width]
                remote(slot, slot, rsx_s.at[0], rsx_r.at[j], partner).wait_recv()
                acc = acc + xbuf[j, :, 0:width]
            wide = 128 + width - V

            def to_z(k):
                return remote(
                    zsend.at[k, :, 0:wide], zbuf.at[k, :, 0:wide], rsz_s.at[k], rsz_r.at[k], at_z(-k)
                )

            for k in range(1, NZ):
                zsend[k, :, 0:128] = acc[:, k * 128:(k + 1) * 128]
                if wide > 128:
                    zsend[k, :, 128:256] = acc[:, V:W]
                to_z(k).start()
            tile = acc[:, 0:128]
            scalar = acc[:, V:W] if wide > 128 else None
            for k in range(1, NZ):
                to_z(k).wait_recv()
                tile = tile + zbuf[k, :, 0:128]
                if wide > 128:
                    scalar = scalar + zbuf[k, :, 128:256]
            tail(gap[...] * rows(d, m)[:, 0:128] + tile, scalar)
            for k in range(1, NZ):
                to_z(k).wait_send()

        for t in range(8):
            @pl.when(8 * c + t != m)
            def _():
                to_chip(t).wait_send()
        pair.wait_send()

    def iterate(step, carry):
        apply_local()

        def tail(tile, scalar):
            def to_z(k):
                return remote(
                    rows(img, m).at[:, 0:128], rows(img, m).at[:, k * 128:(k + 1) * 128],
                    agz_s.at[k], agz_r.at[k], at_z(k),
                )

            rows(img, m)[:, 0:128] = tile
            for k in range(1, NZ):
                to_z(k).start()
            for k in range(1, NZ):
                to_z(k).wait_recv()
            for k in range(1, NZ):
                to_z(k).wait_send()

        reduce(V, tail)
        spread()
        image, trial = img[...], d[...]
        old = rr[0:1, 0:1]
        alpha = old / total(trial * image)
        x[...] = x[...] + alpha * rows(d, m)[:, 0:128]
        left = r[...] - alpha * image
        new = total(left * left)
        r[...] = left
        d[...] = left + (new / old) * trial
        rr[...] = jnp.broadcast_to(new, (8, 128))
        return carry

    lax.fori_loop(0, ITERS - 1, iterate, 0)

    apply_local()
    own_d = rows(d, m)[:, 0:128]
    own_gap = total(gap[...] * own_d * own_d)
    curve = total(d[...] * part[:, 0:V]) + jnp.where(owner, own_gap, jnp.zeros_like(own_gap))
    part[:, V:W] = jnp.broadcast_to(curve, (128, 128))

    def hand(ref):
        return remote(ref, ref, fs.at[0], fs.at[1], partner)

    def last(tile, scalar):
        fin[:, 0:128] = tile
        fin[:, 128:256] = scalar
        hand(fin).start()
        hand(fin).wait_send()

    reduce(W, last)

    @pl.when(jnp.logical_not(owner))
    def _():
        hand(fin).wait_recv()

    alpha = rr[...] / fin[:, 128:256]
    answer = x[...] + alpha * rows(d, m)[:, 0:128]
    left = rows(r, m)[:, 0:128] - alpha * fin[:, 0:128]
    lower = c == 0
    sol[...] = jnp.where(lower, answer[0:4], answer[4:8])
    res[...] = jnp.where(lower, left[0:4], left[4:8])

    for k in ARRIVAL:
        exchange(k).wait_send()


def on_device(integrals, occupied_energy, virtual_energy, right_side):
    dma = pltpu.SemaphoreType.DMA
    vmem = pl.BlockSpec(memory_space=pltpu.VMEM)
    out = jax.ShapeDtypeStruct((4, 128), F32)
    answer, left = pl.pallas_call(
        kernel,
        out_shape=(out, out),
        in_specs=[pl.BlockSpec(memory_space=pl.ANY), pl.BlockSpec(memory_space=pltpu.SMEM), vmem, vmem],
        out_specs=(vmem, vmem),
        scratch_shapes=[
            pltpu.VMEM((NZ, NP, 128, 128), F32),
            pltpu.VMEM((NP * O, V), BF16),
            pltpu.VMEM((NP * O, V), BF16),
            pltpu.VMEM((O, V), F32),
            pltpu.VMEM((O, V), F32),
            pltpu.VMEM((O, V), F32),
            pltpu.VMEM((O, W), F32),
            pltpu.VMEM((64, W), F32),
            pltpu.VMEM((NM, 8, W), F32),
            pltpu.VMEM((NZ, 8, 256), F32),
            pltpu.VMEM((NZ, 8, 256), F32),
            pltpu.VMEM((8, W), F32),
            pltpu.VMEM((8, W), F32),
            pltpu.VMEM((8, 128), F32),
            pltpu.VMEM((8, 128), F32),
            pltpu.VMEM((256, V), BF16),
            pltpu.VMEM((256, NP * O), BF16),
            pltpu.VMEM((8, 128), F32),
            pltpu.VMEM((8, 256), F32),
            dma((NZ,)), dma((NZ,)), dma(()),
            dma((NZ,)), dma((NZ,)), dma((2,)),
            dma((NZ,)), dma((NZ,)), dma((NM,)), dma((8,)), dma((8,)), dma((8,)),
            dma((2,)), dma((8,)), dma((NM,)), dma((NZ,)), dma((NZ,)), dma((2,)),
        ],
        compiler_params=pltpu.CompilerParams(
            collective_id=0, has_side_effects=True, vmem_limit_bytes=60 << 20
        ),
        name="solve",
    )(integrals, occupied_energy, virtual_energy.reshape(1, 128), right_side.T)
    return answer.T, left.T


def solution(mesh):
    in_specs = (P("aux", None, "vir"), P("aux"), P("vir"), P("vir", "aux"))
    out_specs = (P("vir", "aux"), P("vir", "aux"))
    return jax.shard_map(
        on_device, mesh=mesh, in_specs=in_specs, out_specs=out_specs, check_vma=False
    )
```

```python
import functools

import jax
import jax.numpy as jnp
from jax import lax
from jax.experimental import pallas as pl
from jax.experimental.pallas import tpu as pltpu
from jax.sharding import PartitionSpec as P

ITERS = 3
NZ = 8
NM = 16
NP = 16
O = 128
V = 1024
W = V + 128
MESH = pl.DeviceIdType.MESH
F32 = jnp.float32
BF16 = jnp.bfloat16
SHIFT = (0, 1, -1, 2, -2, 3, -3, 4)
ISSUE = (7, 5, 6, 3, 4, 1, 2)
HALF = 512
CHUNKS = 4
NC = NP // CHUNKS
NEAR, FAR = 0, 1


def total(x):
    return jnp.sum(jnp.sum(x, axis=0, keepdims=True), axis=1, keepdims=True)


def split(x):
    high = x.astype(BF16)
    return high, (x - high.astype(F32)).astype(BF16)


def kernel(
    ints, occ, vir, rhs, out,
    recv, bhi, blo, d, r, img, part, cbuf, xbuf, zsend, zbuf, sbuf, g, g2, gap, x, d2, zs, rr, fin,
    a2a_s, a2a_r, loc, iz_s, iz_r, ic, agz_s, agz_r, agx_s, agx_r, agc_s, agc_r,
    rsc_s, rsc_r, rsx_s, rsx_r, rsz_s, rsz_r, sc_s, sc_r, fs,
):
    a = lax.axis_index("aux")
    z = lax.axis_index("vir")
    c = lax.rem(a, 2)
    m = lax.div(a, 2)
    owner = lax.div(m, 8) == c
    partner = (2 * m + 1 - c, z)

    def at_z(k):
        return (a, lax.rem(z + k + NZ, NZ))

    def at_m(chip):
        return (2 * chip + c, z)

    def remote(src, dst, send, recv_sem, dev):
        return pltpu.make_async_remote_copy(
            src_ref=src, dst_ref=dst, send_sem=send, recv_sem=recv_sem, device_id=dev, device_id_type=MESH
        )

    def rows(ref, chip, count=8):
        return ref.at[pl.ds(pl.multiple_of(8 * chip, 8), count)]

    barrier = pltpu.get_barrier_semaphore()
    pl.semaphore_signal(barrier, inc=1, device_id=partner, device_id_type=MESH)
    for k in range(1, NZ):
        pl.semaphore_signal(barrier, inc=1, device_id=at_z(k), device_id_type=MESH)
    for j in range(1, NM):
        pl.semaphore_signal(barrier, inc=1, device_id=at_m(lax.rem(m + j, NM)), device_id_type=MESH)

    row = lax.broadcasted_iota(jnp.int32, (8, 128), 0)
    mine = lax.div(row, 4) == c
    occ_rows = jnp.zeros((8, 128), F32)
    for i in range(4):
        occ_rows = jnp.where(lax.rem(row, 4) == i, occ[i], occ_rows)
    own = rhs[...]
    g[:, 0:128] = jnp.where(mine, jnp.concatenate([own, own], axis=0), 0.0)
    g[:, V:W] = jnp.where(mine, jnp.broadcast_to(vir[...], (8, 128)) - occ_rows, 0.0)

    pl.semaphore_wait(barrier, 1 + NZ - 1 + NM - 1)

    def init_z(q):
        return remote(g.at[:, 0:128], g.at[:, q * 128:(q + 1) * 128], iz_s.at[q], iz_r.at[q], at_z(SHIFT[q]))

    def exchange(q, n):
        to = lax.rem(z + SHIFT[q] + NZ, NZ)
        return remote(
            ints.at[pl.ds(to * NP + n * NC, NC)], recv.at[q, pl.ds(n * NC, NC)], a2a_s.at[q, n], a2a_r.at[q, n], (a, to)
        )

    for q in range(1, NZ):
        init_z(q).start()
    for n in range(CHUNKS):
        for q in ISSUE:
            exchange(q, n).start()
    local = pltpu.make_async_copy(ints.at[pl.ds(z * NP, NP)], recv.at[0], loc)
    local.start()

    def spread(ready):
        def piece(chip, h):
            return rows(img, chip).at[:, h * HALF:(h + 1) * HALF]

        def to_chip(j, h):
            return remote(
                piece(m, h), piece(m, h), agx_s.at[h, j], agx_r.at[h, lax.rem(m, 8)], at_m(lax.rem(m + j, NM))
            )

        def to_partner(t, h):
            block = piece(8 * c + t, h)
            return remote(block, block, agc_s.at[h, t], agc_r.at[h, t], partner)

        def from_partner(t, h):
            block = piece(8 * (1 - c) + t, h)
            return remote(block, block, agc_s.at[h, t], agc_r.at[h, t], partner)

        @pl.when(owner)
        def _():
            for h in (NEAR, FAR):
                ready(h)
                for j in range(1, NM):
                    to_chip(j, h).start()
                to_partner(lax.rem(m, 8), h).start()

        for h in (NEAR, FAR):
            for t in range(8):
                @pl.when(8 * c + t != m)
                def _():
                    block = piece(8 * c + t, h)
                    remote(block, block, agx_s.at[0, 0], agx_r.at[h, t], partner).wait_recv()
                    to_partner(t, h).start()

        for h in (NEAR, FAR):
            for t in range(8):
                from_partner(t, h).wait_recv()
        for h in (NEAR, FAR):
            for t in range(8):
                to_partner(t, h).wait_send()

        @pl.when(owner)
        def _():
            for h in (NEAR, FAR):
                for j in range(1, NM):
                    to_chip(j, h).wait_send()

    for q in range(1, NZ):
        init_z(q).wait_recv()
    swap = remote(g, g2, ic.at[0], ic.at[1], partner)
    swap.start()
    swap.wait_recv()
    gap[...] = g[:, V:W] + g2[:, V:W]

    @pl.when(owner)
    def _():
        rows(img, m)[...] = g[:, 0:V] + g2[:, 0:V]

    spread(lambda h: None)
    swap.wait_send()
    for q in range(1, NZ):
        init_z(q).wait_send()

    first = img[...]
    d[...] = first
    r[...] = first
    rr[...] = jnp.broadcast_to(total(first * first), (8, 128))
    x[...] = jnp.zeros((8, 128), F32)

    def set_trial():
        high, low = split(d[...])
        d2[0:128, :] = high
        d2[128:256, :] = low

    def inter(n, carry):
        eye = lax.broadcasted_iota(jnp.int32, (128, 128), 0) == lax.broadcasted_iota(jnp.int32, (128, 128), 1)
        contract = (((1,), (1,)), ((), ()))
        size = NC * O
        at = pl.ds(pl.multiple_of(n * size, size), size)
        both = lax.dot_general(bhi[at, :], d2[...], contract, preferred_element_type=F32)
        rest = lax.dot_general(blo[at, :], d2[0:128, :], contract, preferred_element_type=F32)
        y = both[:, 0:128] + both[:, 128:256] + rest
        for i in range(NC):
            block = y[i * 128:(i + 1) * 128, :]
            coulomb = total(jnp.where(eye, block, 0.0))
            zh, zl = split(jnp.where(eye, 4.0 * coulomb, 0.0) - block)
            cols = pl.ds(pl.multiple_of(n * size + i * 128, 128), 128)
            zs[0:128, cols] = zh
            zs[128:256, cols] = zl
        return carry

    def outer(h):
        def body(n, carry):
            cols = pl.ds(pl.multiple_of(h * HALF + n * 256, 256), 256)
            to = pl.ds(pl.multiple_of(h * (HALF + 128) + n * 256, 128), 256)
            both = jnp.dot(zs[...], bhi[:, cols], preferred_element_type=F32)
            rest = jnp.dot(zs[0:128, :], blo[:, cols], preferred_element_type=F32)
            part[:, to] = both[0:128] + both[128:256] + rest
            return carry

        lax.fori_loop(0, HALF // 256, body, 0)

    set_trial()
    local.wait()

    def arrive(n, carry):
        for q in ISSUE:
            exchange(q, n).wait_recv()

        def body(i, carry):
            p = n * NC + i
            at = pl.ds(pl.multiple_of(p * 128, 128), 128)
            for q in range(NZ):
                high, low = split(recv[q, p])
                bhi[at, q * 128:(q + 1) * 128] = high
                blo[at, q * 128:(q + 1) * 128] = low
            return carry

        lax.fori_loop(0, NC, body, 0)
        return inter(n, carry)

    lax.fori_loop(0, CHUNKS, arrive, 0)

    def span(h, scalar):
        if h == FAR:
            return slice(HALF + 128, W)
        return slice(0, HALF + 128 if scalar else HALF)

    def reduce(before, tail, scalar):
        def pair(h):
            cols = span(h, scalar)
            theirs = rows(part, 8 * (1 - c), 64).at[:, cols]
            return remote(theirs, cbuf.at[:, cols], rsc_s.at[h], rsc_r.at[h], partner)

        def to_chip(t, h):
            chip = 8 * c + t
            j = lax.rem(chip - m + NM, NM)
            cols = span(h, scalar)
            return remote(
                rows(part, chip).at[:, cols], xbuf.at[j, :, cols], rsx_s.at[h, t], rsx_r.at[h, j], at_m(chip)
            )

        def to_z(q):
            return remote(zsend.at[q], zbuf.at[q], rsz_s.at[q], rsz_r.at[q], at_z(-SHIFT[q]))

        def scalar_z(q):
            return remote(zsend.at[0], sbuf.at[q], sc_s.at[q], sc_r.at[q], at_z(-SHIFT[q]))

        for h in (FAR, NEAR):
            outer(h)
            if h == NEAR:
                before()
            pair(h).start()
        for h in (FAR, NEAR):
            pair(h).wait_recv()
            cols = span(h, scalar)
            half = rows(part, 8 * c, 64)
            half[:, cols] = half[:, cols] + cbuf[:, cols]
            for t in range(8):
                @pl.when(8 * c + t != m)
                def _():
                    to_chip(t, h).start()

        @pl.when(owner)
        def _():
            for h in (FAR, NEAR):
                cols = span(h, scalar)
                acc = rows(part, m)[:, cols]
                for j in range(1, NM):
                    slot = xbuf.at[j, :, cols]
                    remote(slot, slot, rsx_s.at[0, 0], rsx_r.at[h, j], partner).wait_recv()
                    acc = acc + xbuf[j, :, cols]
                if scalar and h == NEAR:
                    zsend[0] = acc[:, HALF:HALF + 128]
                    for q in range(NZ - 1, 0, -1):
                        scalar_z(q).start()
                for q in range(4 * h + 3, 4 * h - 1, -1):
                    if q > 0:
                        zsend[q] = acc[:, (q - 4 * h) * 128:(q - 4 * h + 1) * 128]
                        to_z(q).start()
            tile = acc[:, 0:128]
            for q in range(1, NZ):
                to_z(q).wait_recv()
                tile = tile + zbuf[q]
            if scalar:
                curve = acc[:, HALF:HALF + 128]
                for q in range(1, NZ):
                    scalar_z(q).wait_recv()
                    curve = curve + sbuf[q]
            else:
                curve = None
            tail(gap[...] * rows(d, m)[:, 0:128] + tile, curve)
            for q in range(1, NZ):
                to_z(q).wait_send()
            if scalar:
                for q in range(1, NZ):
                    scalar_z(q).wait_send()

        for h in (FAR, NEAR):
            for t in range(8):
                @pl.when(8 * c + t != m)
                def _():
                    to_chip(t, h).wait_send()
            pair(h).wait_send()

    def iterate(step, carry):
        def to_z(q):
            return remote(
                rows(img, m).at[:, 0:128], rows(img, m).at[:, q * 128:(q + 1) * 128],
                agz_s.at[q], agz_r.at[q], at_z(SHIFT[q]),
            )

        def tail(tile, curve):
            rows(img, m)[:, 0:128] = tile
            for q in range(NZ - 1, 0, -1):
                to_z(q).start()

        def ready(h):
            for q in range(4 * h, 4 * h + 4):
                if q > 0:
                    to_z(q).wait_recv()

        reduce(lambda: None, tail, False)
        spread(ready)

        @pl.when(owner)
        def _():
            for q in range(1, NZ):
                to_z(q).wait_send()

        image, trial = img[...], d[...]
        old = rr[0:1, 0:1]
        alpha = old / total(trial * image)
        x[...] = x[...] + alpha * rows(d, m)[:, 0:128]
        left = r[...] - alpha * image
        new = total(left * left)
        r[...] = left
        d[...] = left + (new / old) * trial
        rr[...] = jnp.broadcast_to(new, (8, 128))
        set_trial()
        lax.fori_loop(0, CHUNKS, inter, 0)
        return carry

    lax.fori_loop(0, ITERS - 1, iterate, 0)

    def add_curvature():
        own_d = rows(d, m)[:, 0:128]
        own_gap = total(gap[...] * own_d * own_d)
        curve = total(d[:, 0:HALF] * part[:, 0:HALF]) + total(d[:, HALF:V] * part[:, HALF + 128:W])
        curve = curve + jnp.where(owner, own_gap, jnp.zeros_like(own_gap))
        part[:, HALF:HALF + 128] = jnp.broadcast_to(curve, (128, 128))

    def hand(ref):
        return remote(ref, ref, fs.at[0], fs.at[1], partner)

    def last(tile, curve):
        fin[:, 0:128] = tile
        fin[:, 128:256] = curve
        hand(fin).start()
        hand(fin).wait_send()

    reduce(add_curvature, last, True)

    @pl.when(jnp.logical_not(owner))
    def _():
        hand(fin).wait_recv()

    alpha = rr[...] / fin[:, 128:256]
    answer = x[...] + alpha * rows(d, m)[:, 0:128]
    left = rows(r, m)[:, 0:128] - alpha * fin[:, 0:128]
    lower = c == 0
    out[0] = jnp.where(lower, answer[0:4], answer[4:8])
    out[1] = jnp.where(lower, left[0:4], left[4:8])

    for n in range(CHUNKS):
        for q in ISSUE:
            exchange(q, n).wait_send()


def on_device(integrals, occupied_energy, virtual_energy, right_side):
    dma = pltpu.SemaphoreType.DMA
    vmem = pl.BlockSpec(memory_space=pltpu.VMEM)
    result = pl.pallas_call(
        kernel,
        out_shape=jax.ShapeDtypeStruct((2, 4, 128), F32),
        in_specs=[pl.BlockSpec(memory_space=pl.ANY), pl.BlockSpec(memory_space=pltpu.SMEM), vmem, vmem],
        out_specs=vmem,
        scratch_shapes=[
            pltpu.VMEM((NZ, NP, 128, 128), F32),
            pltpu.VMEM((NP * O, V), BF16),
            pltpu.VMEM((NP * O, V), BF16),
            pltpu.VMEM((O, V), F32),
            pltpu.VMEM((O, V), F32),
            pltpu.VMEM((O, V), F32),
            pltpu.VMEM((O, W), F32),
            pltpu.VMEM((64, W), F32),
            pltpu.VMEM((NM, 8, W), F32),
            pltpu.VMEM((NZ, 8, 128), F32),
            pltpu.VMEM((NZ, 8, 128), F32),
            pltpu.VMEM((NZ, 8, 128), F32),
            pltpu.VMEM((8, W), F32),
            pltpu.VMEM((8, W), F32),
            pltpu.VMEM((8, 128), F32),
            pltpu.VMEM((8, 128), F32),
            pltpu.VMEM((256, V), BF16),
            pltpu.VMEM((256, NP * O), BF16),
            pltpu.VMEM((8, 128), F32),
            pltpu.VMEM((8, 256), F32),
            dma((NZ, CHUNKS)), dma((NZ, CHUNKS)), dma(()),
            dma((NZ,)), dma((NZ,)), dma((2,)),
            dma((NZ,)), dma((NZ,)), dma((2, NM)), dma((2, 8)), dma((2, 8)), dma((2, 8)),
            dma((2,)), dma((2,)), dma((2, 8)), dma((2, NM)), dma((NZ,)), dma((NZ,)), dma((NZ,)), dma((NZ,)), dma((2,)),
        ],
        compiler_params=pltpu.CompilerParams(
            collective_id=0, has_side_effects=True, vmem_limit_bytes=60 << 20
        ),
        name="solve",
    )(integrals, occupied_energy, virtual_energy.reshape(1, 128), right_side.T)
    return result[0].T, result[1].T


def solution(mesh):
    in_specs = (P("aux", None, "vir"), P("aux"), P("vir"), P("vir", "aux"))
    out_specs = (P("vir", "aux"), P("vir", "aux"))
    return jax.shard_map(
        on_device, mesh=mesh, in_specs=in_specs, out_specs=out_specs, check_vma=False
    )
```

```python
import functools

import jax
import jax.numpy as jnp
from jax import lax
from jax.experimental import pallas as pl
from jax.experimental.pallas import tpu as pltpu
from jax.sharding import PartitionSpec as P

ITERS = 3
NZ = 8
NM = 16
NP = 16
O = 128
V = 1024
W = V + 128
MESH = pl.DeviceIdType.MESH
F32 = jnp.float32
BF16 = jnp.bfloat16
SHIFT = (0, 1, -1, 2, -2, 3, -3, 4)
ISSUE = (7, 5, 6, 3, 4, 1, 2)
HALF = 512
CHUNKS = 8
NC = NP // CHUNKS


def total(x):
    return jnp.sum(jnp.sum(x, axis=0, keepdims=True), axis=1, keepdims=True)


def split(x):
    high = x.astype(BF16)
    return high, (x - high.astype(F32)).astype(BF16)


def kernel(
    ints, occ_in, vir_in, rhs_in, out,
    occ, vir, rhs, recv, bhi, blo, d, r, img, part, cbuf, xbuf, zbuf, zsend, tbuf, sbuf, g, g2, gap, x, d2, zs, rr, fin,
    a2a_s, a2a_r, loc, iz_s, iz_r, ic, agx_s, agx_r, agc_s, agc_r,
    rsc_s, rsc_r, rsx_s, rsx_r, zz_s, zz_r, rsz_s, rsz_r, sc_s, sc_r, fs,
):
    a = lax.axis_index("aux")
    z = lax.axis_index("vir")
    c = lax.rem(a, 2)
    m = lax.div(a, 2)
    owner = lax.div(m, 8) == c
    partner = (2 * m + 1 - c, z)

    def at_z(k):
        return (a, lax.rem(z + k + NZ, NZ))

    def at_m(chip):
        return (2 * chip + c, z)

    def remote(src, dst, send, recv_sem, dev):
        return pltpu.make_async_remote_copy(
            src_ref=src, dst_ref=dst, send_sem=send, recv_sem=recv_sem, device_id=dev, device_id_type=MESH
        )

    def rows(ref, chip, count=8):
        return ref.at[pl.ds(pl.multiple_of(8 * chip, 8), count)]

    barrier = pltpu.get_barrier_semaphore()
    pl.semaphore_signal(barrier, inc=1, device_id=partner, device_id_type=MESH)
    for k in range(1, NZ):
        pl.semaphore_signal(barrier, inc=1, device_id=at_z(k), device_id_type=MESH)
    for j in range(1, NM):
        pl.semaphore_signal(barrier, inc=1, device_id=at_m(lax.rem(m + j, NM)), device_id_type=MESH)

    small = [
        pltpu.make_async_copy(source, target, loc.at[i])
        for i, (source, target) in enumerate(((occ_in, occ), (vir_in, vir), (rhs_in, rhs)), 1)
    ]
    for copy in small:
        copy.start()
    here = pl.ds(pl.multiple_of(z * 128, 128), 128)
    for copy in small:
        copy.wait()

    row = lax.broadcasted_iota(jnp.int32, (8, 128), 0)
    mine = lax.div(row, 4) == c
    occ_rows = jnp.zeros((8, 128), F32)
    for i in range(4):
        occ_rows = jnp.where(lax.rem(row, 4) == i, occ[i], occ_rows)
    own = rhs[...]
    g[0, :, here] = jnp.where(mine, jnp.concatenate([own, own], axis=0), 0.0)
    g[1, :, here] = jnp.where(mine, jnp.broadcast_to(vir[...], (8, 128)) - occ_rows, 0.0)

    pl.semaphore_wait(barrier, 1 + NZ - 1 + NM - 1)

    def init_z(q):
        tile = g.at[:, :, here]
        return remote(tile, tile, iz_s.at[q], iz_r.at[q], at_z(SHIFT[q]))

    def exchange(q, n):
        to = lax.rem(z + SHIFT[q] + NZ, NZ)
        return remote(
            ints.at[pl.ds(to * NP + n * NC, NC)], recv.at[z, pl.ds(n * NC, NC)], a2a_s.at[q, n], a2a_r.at[q, n], (a, to)
        )

    for q in range(1, NZ):
        init_z(q).start()
    for n in range(CHUNKS):
        for q in ISSUE:
            exchange(q, n).start()
    local = pltpu.make_async_copy(ints.at[pl.ds(z * NP, NP)], recv.at[z], loc.at[0])
    local.start()

    def spread(ready):
        def piece(chip, h):
            return rows(img, chip).at[:, h * HALF:(h + 1) * HALF]

        def to_chip(j, h):
            return remote(
                piece(m, h), piece(m, h), agx_s.at[h, j], agx_r.at[h, lax.rem(m, 8)], at_m(lax.rem(m + j, NM))
            )

        def to_partner(t, h):
            block = piece(8 * c + t, h)
            return remote(block, block, agc_s.at[h, t], agc_r.at[h, t], partner)

        def from_partner(t, h):
            block = piece(8 * (1 - c) + t, h)
            return remote(block, block, agc_s.at[h, t], agc_r.at[h, t], partner)

        @pl.when(owner)
        def _():
            for h in range(2):
                ready(h)
                for j in range(1, NM):
                    to_chip(j, h).start()
                to_partner(lax.rem(m, 8), h).start()

        for h in range(2):
            for t in range(8):
                @pl.when(8 * c + t != m)
                def _():
                    block = piece(8 * c + t, h)
                    remote(block, block, agx_s.at[0, 0], agx_r.at[h, t], partner).wait_recv()
                    to_partner(t, h).start()

        for h in range(2):
            for t in range(8):
                from_partner(t, h).wait_recv()
        for h in range(2):
            for t in range(8):
                to_partner(t, h).wait_send()

        @pl.when(owner)
        def _():
            for h in range(2):
                for j in range(1, NM):
                    to_chip(j, h).wait_send()

    for q in range(1, NZ):
        init_z(q).wait_recv()
    swap = remote(g, g2, ic.at[0], ic.at[1], partner)
    swap.start()
    swap.wait_recv()
    gap[...] = g[1] + g2[1]

    @pl.when(owner)
    def _():
        rows(img, m)[...] = g[0] + g2[0]

    spread(lambda h: None)
    swap.wait_send()
    for q in range(1, NZ):
        init_z(q).wait_send()

    first = img[...]
    d[...] = first
    r[...] = first
    rr[...] = jnp.broadcast_to(total(first * first), (8, 128))
    x[...] = jnp.zeros((8, 128), F32)

    def set_trial():
        high, low = split(d[...])
        d2[0:128, :] = high
        d2[128:256, :] = low

    def inter(n, count):
        eye = lax.broadcasted_iota(jnp.int32, (128, 128), 0) == lax.broadcasted_iota(jnp.int32, (128, 128), 1)
        contract = (((1,), (1,)), ((), ()))
        size = count * O
        at = pl.ds(pl.multiple_of(n * size, size), size)
        both = lax.dot_general(bhi[at, :], d2[...], contract, preferred_element_type=F32)
        rest = lax.dot_general(blo[at, :], d2[0:128, :], contract, preferred_element_type=F32)
        y = both[:, 0:128] + both[:, 128:256] + rest
        for i in range(count):
            block = y[i * 128:(i + 1) * 128, :]
            coulomb = total(jnp.where(eye, block, 0.0))
            zh, zl = split(jnp.where(eye, 4.0 * coulomb, 0.0) - block)
            cols = pl.ds(pl.multiple_of(n * size + i * 128, 128), 128)
            zs[0:128, cols] = zh
            zs[128:256, cols] = zl

    def outer(h):
        def body(n, carry):
            cols = pl.ds(pl.multiple_of(h * HALF + n * 256, 256), 256)
            to = pl.ds(pl.multiple_of(h * HALF + n * 256, 256), 256)
            both = jnp.dot(zs[...], bhi[:, cols], preferred_element_type=F32)
            rest = jnp.dot(zs[0:128, :], blo[:, cols], preferred_element_type=F32)
            part[:, to] = both[0:128] + both[128:256] + rest
            return carry

        lax.fori_loop(0, HALF // 256, body, 0)

    set_trial()
    local.wait()

    def arrive(n, carry):
        for q in ISSUE:
            exchange(q, n).wait_recv()

        def body(i, carry):
            p = n * NC + i
            at = pl.ds(pl.multiple_of(p * 128, 128), 128)
            for q in range(NZ):
                high, low = split(recv[q, p])
                bhi[at, q * 128:(q + 1) * 128] = high
                blo[at, q * 128:(q + 1) * 128] = low
            return carry

        lax.fori_loop(0, NC, body, 0)
        inter(n, NC)
        return carry

    lax.fori_loop(0, CHUNKS, arrive, 0)

    def span(h, scalar):
        return slice(h * HALF, W if h == 1 and scalar else (h + 1) * HALF)

    def reduce(before, collect, scalar):
        def pair(h):
            cols = span(h, scalar)
            theirs = rows(part, 8 * (1 - c), 64).at[:, cols]
            return remote(theirs, cbuf.at[:, cols], rsc_s.at[h], rsc_r.at[h], partner)

        def to_chip(t, h):
            chip = 8 * c + t
            j = lax.rem(chip - m + NM, NM)
            cols = span(h, scalar)
            return remote(
                rows(part, chip).at[:, cols], xbuf.at[j, :, cols], rsx_s.at[h, t], rsx_r.at[h, j], at_m(chip)
            )

        for h in range(2):
            outer(h)
            if h == 1:
                before()
            pair(h).start()
        for h in range(2):
            pair(h).wait_recv()
            cols = span(h, scalar)
            half = rows(part, 8 * c, 64)
            half[:, cols] = half[:, cols] + cbuf[:, cols]
            for t in range(8):
                @pl.when(8 * c + t != m)
                def _():
                    to_chip(t, h).start()

        @pl.when(owner)
        def _():
            for h in range(2):
                cols = span(h, scalar)
                acc = rows(part, m)[:, cols]
                for j in range(1, NM):
                    slot = xbuf.at[j, :, cols]
                    remote(slot, slot, rsx_s.at[0, 0], rsx_r.at[h, j], partner).wait_recv()
                    acc = acc + xbuf[j, :, cols]
                collect(h, acc)

        def finish():
            for h in range(2):
                for t in range(8):
                    @pl.when(8 * c + t != m)
                    def _():
                        to_chip(t, h).wait_send()
                pair(h).wait_send()

        return finish

    def iterate(step, carry):
        slot = lax.rem(step, 2)

        def to_z(q, h):
            block = zbuf.at[slot, z, :, h * HALF:(h + 1) * HALF]
            return remote(block, block, zz_s.at[slot, h, q], zz_r.at[slot, h, q], at_z(SHIFT[q]))

        def collect(h, acc):
            zbuf[slot, z, :, h * HALF:(h + 1) * HALF] = acc
            for q in ISSUE:
                to_z(q, h).start()

        def ready(h):
            cols = slice(h * HALF, (h + 1) * HALF)
            for q in range(1, NZ):
                to_z(q, h).wait_recv()
            acc = gap[:, cols] * rows(d, m)[:, cols]
            for s in range(NZ):
                acc = acc + zbuf[slot, s, :, cols]
            rows(img, m)[:, cols] = acc

        finish = reduce(lambda: None, collect, False)
        spread(ready)
        finish()

        @pl.when(owner)
        def _():
            for h in range(2):
                for q in range(1, NZ):
                    to_z(q, h).wait_send()

        image, trial = img[...], d[...]
        old = rr[0:1, 0:1]
        alpha = old / total(trial * image)
        x[...] = x[...] + alpha * rows(d, m)[:, here]
        left = r[...] - alpha * image
        new = total(left * left)
        r[...] = left
        d[...] = left + (new / old) * trial
        rr[...] = jnp.broadcast_to(new, (8, 128))
        set_trial()
        lax.fori_loop(0, NP // 4, lambda n, carry: inter(n, 4) or carry, 0)
        return carry

    lax.fori_loop(0, ITERS - 1, iterate, 0)

    own_d = rows(d, m)[:, here]

    def add_curvature():
        own_gap = total(gap[:, here] * own_d * own_d)
        curve = total(d[...] * part[:, 0:V]) + jnp.where(owner, own_gap, jnp.zeros_like(own_gap))
        part[:, V:W] = jnp.broadcast_to(curve, (128, 128))

    def tile_z(q):
        to = lax.rem(z + SHIFT[q] + NZ, NZ)
        return remote(zsend.at[to], tbuf.at[q], rsz_s.at[q], rsz_r.at[q], (a, to))

    def scalar_z(q):
        return remote(zsend.at[NZ], sbuf.at[q], sc_s.at[q], sc_r.at[q], at_z(SHIFT[q]))

    def hand(ref):
        return remote(ref, ref, fs.at[0], fs.at[1], partner)

    def last(h, acc):
        for s in range(4):
            zsend[4 * h + s] = acc[:, s * 128:(s + 1) * 128]
        if h == 0:
            return
        zsend[NZ] = acc[:, HALF:HALF + 128]
        for q in ISSUE:
            scalar_z(q).start()
            tile_z(q).start()
        tile = gap[:, here] * own_d + zsend[z]
        curve = zsend[NZ]
        for q in range(1, NZ):
            tile_z(q).wait_recv()
            scalar_z(q).wait_recv()
            tile = tile + tbuf[q]
            curve = curve + sbuf[q]
        fin[:, 0:128] = tile
        fin[:, 128:256] = curve
        hand(fin).start()
        for q in range(1, NZ):
            tile_z(q).wait_send()
            scalar_z(q).wait_send()
        hand(fin).wait_send()

    reduce(add_curvature, last, True)()

    @pl.when(jnp.logical_not(owner))
    def _():
        hand(fin).wait_recv()

    alpha = rr[...] / fin[:, 128:256]
    answer = x[...] + alpha * own_d
    left = rows(r, m)[:, here] - alpha * fin[:, 0:128]
    lower = c == 0
    out[0] = jnp.where(lower, answer[0:4], answer[4:8])
    out[1] = jnp.where(lower, left[0:4], left[4:8])

    for n in range(CHUNKS):
        for q in ISSUE:
            exchange(q, n).wait_send()


def on_device(integrals, occupied_energy, virtual_energy, right_side):
    dma = pltpu.SemaphoreType.DMA
    vmem = pl.BlockSpec(memory_space=pltpu.VMEM)
    result = pl.pallas_call(
        kernel,
        out_shape=jax.ShapeDtypeStruct((2, 4, 128), F32),
        in_specs=[pl.BlockSpec(memory_space=pl.ANY)] * 4,
        out_specs=vmem,
        scratch_shapes=[
            pltpu.SMEM((4,), F32),
            pltpu.VMEM((1, 128), F32),
            pltpu.VMEM((4, 128), F32),
            pltpu.VMEM((NZ, NP, 128, 128), F32),
            pltpu.VMEM((NP * O, V), BF16),
            pltpu.VMEM((NP * O, V), BF16),
            pltpu.VMEM((O, V), F32),
            pltpu.VMEM((O, V), F32),
            pltpu.VMEM((O, V), F32),
            pltpu.VMEM((O, W), F32),
            pltpu.VMEM((64, W), F32),
            pltpu.VMEM((NM, 8, W), F32),
            pltpu.VMEM((2, NZ, 8, V), F32),
            pltpu.VMEM((NZ + 1, 8, 128), F32),
            pltpu.VMEM((NZ, 8, 128), F32),
            pltpu.VMEM((NZ, 8, 128), F32),
            pltpu.VMEM((2, 8, V), F32),
            pltpu.VMEM((2, 8, V), F32),
            pltpu.VMEM((8, V), F32),
            pltpu.VMEM((8, 128), F32),
            pltpu.VMEM((256, V), BF16),
            pltpu.VMEM((256, NP * O), BF16),
            pltpu.VMEM((8, 128), F32),
            pltpu.VMEM((8, 256), F32),
            dma((NZ, CHUNKS)), dma((NZ, CHUNKS)), dma((4,)),
            dma((NZ,)), dma((NZ,)), dma((2,)), dma((2, NM)), dma((2, 8)), dma((2, 8)), dma((2, 8)),
            dma((2,)), dma((2,)), dma((2, 8)), dma((2, NM)), dma((2, 2, NZ)), dma((2, 2, NZ)),
            dma((NZ,)), dma((NZ,)), dma((NZ,)), dma((NZ,)), dma((2,)),
        ],
        compiler_params=pltpu.CompilerParams(
            collective_id=0, has_side_effects=True, vmem_limit_bytes=60 << 20
        ),
        name="solve",
    )(integrals, occupied_energy, virtual_energy.reshape(1, 128), right_side.T)
    return result[0].T, result[1].T


def solution(mesh):
    in_specs = (P("aux", None, "vir"), P("aux"), P("vir"), P("vir", "aux"))
    out_specs = (P("vir", "aux"), P("vir", "aux"))
    return jax.shard_map(
        on_device, mesh=mesh, in_specs=in_specs, out_specs=out_specs, check_vma=False
    )
```

```python
import functools

import jax
import jax.numpy as jnp
from jax import lax
from jax.experimental import pallas as pl
from jax.experimental.pallas import tpu as pltpu
from jax.sharding import PartitionSpec as P

ITERS = 3
NZ = 8
NM = 16
NP = 16
O = 128
V = 1024
W = V + 128
MESH = pl.DeviceIdType.MESH
F32 = jnp.float32
BF16 = jnp.bfloat16
SHIFT = (0, 1, -1, 2, -2, 3, -3, 4)
ISSUE = (7, 5, 6, 3, 4, 1, 2)
HALF = 512
CHUNKS = 8
AHEAD = 3
NC = NP // CHUNKS


def total(x):
    return jnp.sum(jnp.sum(x, axis=0, keepdims=True), axis=1, keepdims=True)


def split(x):
    high = x.astype(BF16)
    return high, (x - high.astype(F32)).astype(BF16)


def kernel(
    ints, occ_in, vir_in, rhs_in, out,
    occ, vir, rhs, recv, bhi, blo, d, r, img, part, cbuf, xbuf, zbuf, zsend, tbuf, sbuf, g, g2, gap, x, d2, zs, rr,
    a2a_s, a2a_r, loc, iz_s, iz_r, ic, agx_s, agx_r, agc_s, agc_r,
    rsc_s, rsc_r, rsx_s, rsx_r, zz_s, zz_r, rsz_s, rsz_r, sc_s, sc_r,
):
    a = lax.axis_index("aux")
    z = lax.axis_index("vir")
    c = lax.rem(a, 2)
    m = lax.div(a, 2)
    owner = lax.div(m, 8) == c
    partner = (2 * m + 1 - c, z)

    def at_z(k):
        return (a, lax.rem(z + k + NZ, NZ))

    def at_m(chip):
        return (2 * chip + c, z)

    def remote(src, dst, send, recv_sem, dev):
        return pltpu.make_async_remote_copy(
            src_ref=src, dst_ref=dst, send_sem=send, recv_sem=recv_sem, device_id=dev, device_id_type=MESH
        )

    def rows(ref, chip, count=8):
        return ref.at[pl.ds(pl.multiple_of(8 * chip, 8), count)]

    barrier = pltpu.get_barrier_semaphore()
    pl.semaphore_signal(barrier, inc=1, device_id=partner, device_id_type=MESH)
    for k in range(1, NZ):
        pl.semaphore_signal(barrier, inc=1, device_id=at_z(k), device_id_type=MESH)
    for j in range(1, NM):
        pl.semaphore_signal(barrier, inc=1, device_id=at_m(lax.rem(m + j, NM)), device_id_type=MESH)

    small = [
        pltpu.make_async_copy(source, target, loc.at[i])
        for i, (source, target) in enumerate(((occ_in, occ), (vir_in, vir), (rhs_in, rhs)), 1)
    ]
    for copy in small:
        copy.start()
    here = pl.ds(pl.multiple_of(z * 128, 128), 128)
    for copy in small:
        copy.wait()

    row = lax.broadcasted_iota(jnp.int32, (8, 128), 0)
    mine = lax.div(row, 4) == c
    occ_rows = jnp.zeros((8, 128), F32)
    for i in range(4):
        occ_rows = jnp.where(lax.rem(row, 4) == i, occ[i], occ_rows)
    own = rhs[...]
    g[0, :, here] = jnp.where(mine, jnp.concatenate([own, own], axis=0), 0.0)
    g[1, :, here] = jnp.where(mine, jnp.broadcast_to(vir[...], (8, 128)) - occ_rows, 0.0)

    pl.semaphore_wait(barrier, 1 + NZ - 1 + NM - 1)

    def init_z(q):
        tile = g.at[:, :, here]
        return remote(tile, tile, iz_s.at[q], iz_r.at[q], at_z(SHIFT[q]))

    def exchange(q, n):
        to = lax.rem(z + SHIFT[q] + NZ, NZ)
        return remote(
            ints.at[pl.ds(to * NP + n * NC, NC)], recv.at[z, pl.ds(n * NC, NC)], a2a_s.at[q, n], a2a_r.at[q, n], (a, to)
        )

    for q in range(1, NZ):
        init_z(q).start()
    for n in range(AHEAD):
        for q in ISSUE:
            exchange(q, n).start()
    local = pltpu.make_async_copy(ints.at[pl.ds(z * NP, NP)], recv.at[z], loc.at[0])
    local.start()

    def spread(ready):
        def piece(chip, h):
            return rows(img, chip).at[:, h * HALF:(h + 1) * HALF]

        def to_chip(j, h):
            return remote(
                piece(m, h), piece(m, h), agx_s.at[h, j], agx_r.at[h, lax.rem(m, 8)], at_m(lax.rem(m + j, NM))
            )

        def to_partner(t, h):
            block = piece(8 * c + t, h)
            return remote(block, block, agc_s.at[h, t], agc_r.at[h, t], partner)

        def from_partner(t, h):
            block = piece(8 * (1 - c) + t, h)
            return remote(block, block, agc_s.at[h, t], agc_r.at[h, t], partner)

        @pl.when(owner)
        def _():
            for h in range(2):
                ready(h)
                for j in range(1, NM):
                    to_chip(j, h).start()
                to_partner(lax.rem(m, 8), h).start()

        for h in range(2):
            for t in range(8):
                @pl.when(8 * c + t != m)
                def _():
                    block = piece(8 * c + t, h)
                    remote(block, block, agx_s.at[0, 0], agx_r.at[h, t], partner).wait_recv()
                    to_partner(t, h).start()

        for h in range(2):
            for t in range(8):
                from_partner(t, h).wait_recv()
        for h in range(2):
            for t in range(8):
                to_partner(t, h).wait_send()

        @pl.when(owner)
        def _():
            for h in range(2):
                for j in range(1, NM):
                    to_chip(j, h).wait_send()

    for q in range(1, NZ):
        init_z(q).wait_recv()
    swap = remote(g, g2, ic.at[0], ic.at[1], partner)
    swap.start()
    swap.wait_recv()
    gap[...] = g[1] + g2[1]

    @pl.when(owner)
    def _():
        rows(img, m)[...] = g[0] + g2[0]

    spread(lambda h: None)
    swap.wait_send()
    for q in range(1, NZ):
        init_z(q).wait_send()

    first = img[...]
    d[...] = first
    r[...] = first
    rr[...] = jnp.broadcast_to(total(first * first), (8, 128))
    x[...] = jnp.zeros((8, 128), F32)

    def set_trial():
        high, low = split(d[...])
        d2[0:128, :] = high
        d2[128:256, :] = low

    def inter(n, count):
        eye = lax.broadcasted_iota(jnp.int32, (128, 128), 0) == lax.broadcasted_iota(jnp.int32, (128, 128), 1)
        contract = (((1,), (1,)), ((), ()))
        size = count * O
        at = pl.ds(pl.multiple_of(n * size, size), size)
        both = lax.dot_general(bhi[at, :], d2[...], contract, preferred_element_type=F32)
        rest = lax.dot_general(blo[at, :], d2[0:128, :], contract, preferred_element_type=F32)
        y = both[:, 0:128] + both[:, 128:256] + rest
        for i in range(count):
            block = y[i * 128:(i + 1) * 128, :]
            coulomb = total(jnp.where(eye, block, 0.0))
            zh, zl = split(jnp.where(eye, 4.0 * coulomb, 0.0) - block)
            cols = pl.ds(pl.multiple_of(n * size + i * 128, 128), 128)
            zs[0:128, cols] = zh
            zs[128:256, cols] = zl

    def outer(h):
        def body(n, carry):
            cols = pl.ds(pl.multiple_of(h * HALF + n * 256, 256), 256)
            to = pl.ds(pl.multiple_of(h * HALF + n * 256, 256), 256)
            both = jnp.dot(zs[...], bhi[:, cols], preferred_element_type=F32)
            rest = jnp.dot(zs[0:128, :], blo[:, cols], preferred_element_type=F32)
            part[:, to] = both[0:128] + both[128:256] + rest
            return carry

        lax.fori_loop(0, HALF // 256, body, 0)

    set_trial()
    local.wait()

    def arrive(n, carry):
        for q in ISSUE:
            exchange(q, n).wait_send()

            @pl.when(n + AHEAD < CHUNKS)
            def _():
                exchange(q, n + AHEAD).start()

        for q in ISSUE:
            exchange(q, n).wait_recv()

        def body(i, carry):
            p = n * NC + i
            at = pl.ds(pl.multiple_of(p * 128, 128), 128)
            for q in range(NZ):
                high, low = split(recv[q, p])
                bhi[at, q * 128:(q + 1) * 128] = high
                blo[at, q * 128:(q + 1) * 128] = low
            return carry

        lax.fori_loop(0, NC, body, 0)
        inter(n, NC)
        return carry

    lax.fori_loop(0, CHUNKS, arrive, 0)

    def span(h, scalar):
        return slice(h * HALF, W if h == 1 and scalar else (h + 1) * HALF)

    def reduce(before, collect, scalar):
        def pair(h):
            cols = span(h, scalar)
            theirs = rows(part, 8 * (1 - c), 64).at[:, cols]
            return remote(theirs, cbuf.at[:, cols], rsc_s.at[h], rsc_r.at[h], partner)

        def to_chip(t, h):
            chip = 8 * c + t
            j = lax.rem(chip - m + NM, NM)
            cols = span(h, scalar)
            return remote(
                rows(part, chip).at[:, cols], xbuf.at[j, :, cols], rsx_s.at[h, t], rsx_r.at[h, j], at_m(chip)
            )

        for h in range(2):
            outer(h)
            if h == 1:
                before()
            pair(h).start()
        for h in range(2):
            pair(h).wait_recv()
            cols = span(h, scalar)
            half = rows(part, 8 * c, 64)
            half[:, cols] = half[:, cols] + cbuf[:, cols]
            for t in range(8):
                @pl.when(8 * c + t != m)
                def _():
                    to_chip(t, h).start()

        @pl.when(owner)
        def _():
            for h in range(2):
                cols = span(h, scalar)
                acc = rows(part, m)[:, cols]
                for j in range(1, NM):
                    slot = xbuf.at[j, :, cols]
                    remote(slot, slot, rsx_s.at[0, 0], rsx_r.at[h, j], partner).wait_recv()
                    acc = acc + xbuf[j, :, cols]
                collect(h, acc)

        def finish():
            for h in range(2):
                for t in range(8):
                    @pl.when(8 * c + t != m)
                    def _():
                        to_chip(t, h).wait_send()
                pair(h).wait_send()

        return finish

    def iterate(step, carry):
        slot = lax.rem(step, 2)

        def to_z(q, h):
            block = zbuf.at[slot, z, :, h * HALF:(h + 1) * HALF]
            return remote(block, block, zz_s.at[slot, h, q], zz_r.at[slot, h, q], at_z(SHIFT[q]))

        def collect(h, acc):
            zbuf[slot, z, :, h * HALF:(h + 1) * HALF] = acc
            for q in ISSUE:
                to_z(q, h).start()

        def ready(h):
            cols = slice(h * HALF, (h + 1) * HALF)
            for q in range(1, NZ):
                to_z(q, h).wait_recv()
            acc = gap[:, cols] * rows(d, m)[:, cols]
            for s in range(NZ):
                acc = acc + zbuf[slot, s, :, cols]
            rows(img, m)[:, cols] = acc

        finish = reduce(lambda: None, collect, False)
        spread(ready)
        finish()

        @pl.when(owner)
        def _():
            for h in range(2):
                for q in range(1, NZ):
                    to_z(q, h).wait_send()

        image, trial = img[...], d[...]
        old = rr[0:1, 0:1]
        alpha = old / total(trial * image)
        x[...] = x[...] + alpha * rows(d, m)[:, here]
        left = r[...] - alpha * image
        new = total(left * left)
        r[...] = left
        d[...] = left + (new / old) * trial
        rr[...] = jnp.broadcast_to(new, (8, 128))
        set_trial()
        lax.fori_loop(0, NP // 8, lambda n, carry: inter(n, 8) or carry, 0)
        return carry

    lax.fori_loop(0, ITERS - 1, iterate, 0)

    own_d = rows(d, m)[:, here]

    def add_curvature():
        own_gap = total(gap[:, here] * own_d * own_d)
        curve = total(d[...] * part[:, 0:V]) + jnp.where(owner, own_gap, jnp.zeros_like(own_gap))
        part[:, V:W] = jnp.broadcast_to(curve, (128, 128))

    def to_peers(q, core):
        to = lax.rem(z + SHIFT[q] + NZ, NZ)
        dev = (2 * m + lax.rem(c + core, 2), to)
        return (
            remote(zsend.at[NZ], sbuf.at[q], sc_s.at[core, q], sc_r.at[q], dev),
            remote(zsend.at[to], tbuf.at[q], rsz_s.at[core, q], rsz_r.at[q], dev),
        )

    sends = [(0, 1)] + [(q, core) for q in ISSUE for core in range(2)]

    def last(h, acc):
        for s in range(4):
            zsend[4 * h + s] = acc[:, s * 128:(s + 1) * 128]
        if h == 0:
            return
        zsend[NZ] = acc[:, HALF:HALF + 128]
        for q, core in sends[1:] + sends[:1]:
            for copy in to_peers(q, core):
                copy.start()
        tbuf[0] = zsend[z]
        sbuf[0] = zsend[NZ]

    finish = reduce(add_curvature, last, True)

    @pl.when(jnp.logical_not(owner))
    def _():
        for copy in to_peers(0, 1):
            copy.wait_recv()

    tile = gap[:, here] * own_d + tbuf[0]
    curve = sbuf[0]
    for q in range(1, NZ):
        for copy in to_peers(q, 0):
            copy.wait_recv()
        tile = tile + tbuf[q]
        curve = curve + sbuf[q]

    alpha = rr[...] / curve
    answer = x[...] + alpha * own_d
    left = rows(r, m)[:, here] - alpha * tile
    lower = c == 0
    out[0] = jnp.where(lower, answer[0:4], answer[4:8])
    out[1] = jnp.where(lower, left[0:4], left[4:8])

    finish()

    @pl.when(owner)
    def _():
        for q, core in sends:
            for copy in to_peers(q, core):
                copy.wait_send()


def on_device(integrals, occupied_energy, virtual_energy, right_side):
    dma = pltpu.SemaphoreType.DMA
    vmem = pl.BlockSpec(memory_space=pltpu.VMEM)
    result = pl.pallas_call(
        kernel,
        out_shape=jax.ShapeDtypeStruct((2, 4, 128), F32),
        in_specs=[pl.BlockSpec(memory_space=pl.ANY)] * 4,
        out_specs=vmem,
        scratch_shapes=[
            pltpu.SMEM((4,), F32),
            pltpu.VMEM((1, 128), F32),
            pltpu.VMEM((4, 128), F32),
            pltpu.VMEM((NZ, NP, 128, 128), F32),
            pltpu.VMEM((NP * O, V), BF16),
            pltpu.VMEM((NP * O, V), BF16),
            pltpu.VMEM((O, V), F32),
            pltpu.VMEM((O, V), F32),
            pltpu.VMEM((O, V), F32),
            pltpu.VMEM((O, W), F32),
            pltpu.VMEM((64, W), F32),
            pltpu.VMEM((NM, 8, W), F32),
            pltpu.VMEM((2, NZ, 8, V), F32),
            pltpu.VMEM((NZ + 1, 8, 128), F32),
            pltpu.VMEM((NZ, 8, 128), F32),
            pltpu.VMEM((NZ, 8, 128), F32),
            pltpu.VMEM((2, 8, V), F32),
            pltpu.VMEM((2, 8, V), F32),
            pltpu.VMEM((8, V), F32),
            pltpu.VMEM((8, 128), F32),
            pltpu.VMEM((256, V), BF16),
            pltpu.VMEM((256, NP * O), BF16),
            pltpu.VMEM((8, 128), F32),
            dma((NZ, CHUNKS)), dma((NZ, CHUNKS)), dma((4,)),
            dma((NZ,)), dma((NZ,)), dma((2,)), dma((2, NM)), dma((2, 8)), dma((2, 8)), dma((2, 8)),
            dma((2,)), dma((2,)), dma((2, 8)), dma((2, NM)), dma((2, 2, NZ)), dma((2, 2, NZ)),
            dma((2, NZ)), dma((NZ,)), dma((2, NZ)), dma((NZ,)),
        ],
        compiler_params=pltpu.CompilerParams(
            collective_id=0, has_side_effects=True, vmem_limit_bytes=60 << 20
        ),
        name="solve",
    )(integrals, occupied_energy, virtual_energy.reshape(1, 128), right_side.T)
    return result[0].T, result[1].T


def solution(mesh):
    in_specs = (P("aux", None, "vir"), P("aux"), P("vir"), P("vir", "aux"))
    out_specs = (P("vir", "aux"), P("vir", "aux"))
    return jax.shard_map(
        on_device, mesh=mesh, in_specs=in_specs, out_specs=out_specs, check_vma=False
    )
```

```python
import functools

import jax
import jax.numpy as jnp
from jax import lax
from jax.experimental import pallas as pl
from jax.experimental.pallas import tpu as pltpu
from jax.sharding import PartitionSpec as P

ITERS = 3
NZ = 8
NM = 16
NP = 16
O = 128
V = 1024
W = V + 128
MESH = pl.DeviceIdType.MESH
F32 = jnp.float32
BF16 = jnp.bfloat16
SHIFT = (0, 1, -1, 2, -2, 3, -3, 4)
ISSUE = (7, 5, 6, 3, 4, 1, 2)
HALF = 512
CHUNKS = 8
AHEAD = 3
NC = NP // CHUNKS


def total(x):
    return jnp.sum(jnp.sum(x, axis=0, keepdims=True), axis=1, keepdims=True)


def split(x):
    high = x.astype(BF16)
    return high, (x - high.astype(F32)).astype(BF16)


def kernel(
    ints, occ_in, vir_in, rhs_in, out,
    occ, vir, rhs, recv, bhi, blo, d, r, img, part, cbuf, xbuf, zbuf, zsend, tbuf, sbuf, g, g2, gap, x, d2, zs, rr,
    a2a_s, a2a_r, loc, iz_s, iz_r, ic, agx_s, agx_r, agc_s, agc_r,
    rsc_s, rsc_r, rsx_s, rsx_r, zz_s, zz_r, rsz_s, rsz_r, sc_s, sc_r,
):
    a = lax.axis_index("aux")
    z = lax.axis_index("vir")
    c = lax.rem(a, 2)
    m = lax.div(a, 2)
    owner = lax.div(m, 8) == c
    partner = (2 * m + 1 - c, z)

    def at_z(k):
        return (a, lax.rem(z + k + NZ, NZ))

    def at_m(chip):
        return (2 * chip + c, z)

    def remote(src, dst, send, recv_sem, dev):
        return pltpu.make_async_remote_copy(
            src_ref=src, dst_ref=dst, send_sem=send, recv_sem=recv_sem, device_id=dev, device_id_type=MESH
        )

    def rows(ref, chip, count=8):
        return ref.at[pl.ds(pl.multiple_of(8 * chip, 8), count)]

    barrier = pltpu.get_barrier_semaphore()
    pl.semaphore_signal(barrier, inc=1, device_id=partner, device_id_type=MESH)
    for k in range(1, NZ):
        pl.semaphore_signal(barrier, inc=1, device_id=at_z(k), device_id_type=MESH)
    for j in range(1, NM):
        pl.semaphore_signal(barrier, inc=1, device_id=at_m(lax.rem(m + j, NM)), device_id_type=MESH)

    small = [
        pltpu.make_async_copy(source, target, loc.at[i])
        for i, (source, target) in enumerate(((occ_in, occ), (vir_in, vir), (rhs_in, rhs)), 1)
    ]
    for copy in small:
        copy.start()
    here = pl.ds(pl.multiple_of(z * 128, 128), 128)
    for copy in small:
        copy.wait()

    row = lax.broadcasted_iota(jnp.int32, (8, 128), 0)
    mine = lax.div(row, 4) == c
    occ_rows = jnp.zeros((8, 128), F32)
    for i in range(4):
        occ_rows = jnp.where(lax.rem(row, 4) == i, occ[i], occ_rows)
    own = rhs[...]
    g[0, :, here] = jnp.where(mine, jnp.concatenate([own, own], axis=0), 0.0)
    g[1, :, here] = jnp.where(mine, jnp.broadcast_to(vir[...], (8, 128)) - occ_rows, 0.0)

    pl.semaphore_wait(barrier, 1 + NZ - 1 + NM - 1)

    def init_z(q):
        tile = g.at[:, :, here]
        return remote(tile, tile, iz_s.at[q], iz_r.at[q], at_z(SHIFT[q]))

    def exchange(q, n):
        to = lax.rem(z + SHIFT[q] + NZ, NZ)
        return remote(
            ints.at[pl.ds(to * NP + n * NC, NC)], recv.at[z, pl.ds(n * NC, NC)], a2a_s.at[q, n], a2a_r.at[q, n], (a, to)
        )

    for q in range(1, NZ):
        init_z(q).start()
    for n in range(AHEAD):
        for q in ISSUE:
            exchange(q, n).start()
    local = pltpu.make_async_copy(ints.at[pl.ds(z * NP, NP)], recv.at[z], loc.at[0])
    local.start()

    def spread(ready):
        def piece(chip, h):
            return rows(img, chip).at[:, h * HALF:(h + 1) * HALF]

        def to_chip(j, h):
            return remote(
                piece(m, h), piece(m, h), agx_s.at[h, j], agx_r.at[h, lax.rem(m, 8)], at_m(lax.rem(m + j, NM))
            )

        def to_partner(t, h):
            block = piece(8 * c + t, h)
            return remote(block, block, agc_s.at[h, t], agc_r.at[h, t], partner)

        def from_partner(t, h):
            block = piece(8 * (1 - c) + t, h)
            return remote(block, block, agc_s.at[h, t], agc_r.at[h, t], partner)

        @pl.when(owner)
        def _():
            for h in range(2):
                ready(h)
                for j in range(1, NM):
                    to_chip(j, h).start()
                to_partner(lax.rem(m, 8), h).start()

        for h in range(2):
            for t in range(8):
                @pl.when(8 * c + t != m)
                def _():
                    block = piece(8 * c + t, h)
                    remote(block, block, agx_s.at[0, 0], agx_r.at[h, t], partner).wait_recv()
                    to_partner(t, h).start()

        for h in range(2):
            for t in range(8):
                from_partner(t, h).wait_recv()
        for h in range(2):
            for t in range(8):
                to_partner(t, h).wait_send()

        @pl.when(owner)
        def _():
            for h in range(2):
                for j in range(1, NM):
                    to_chip(j, h).wait_send()

    for q in range(1, NZ):
        init_z(q).wait_recv()
    swap = remote(g, g2, ic.at[0], ic.at[1], partner)
    swap.start()
    swap.wait_recv()
    gap[...] = g[1] + g2[1]

    @pl.when(owner)
    def _():
        rows(img, m)[...] = g[0] + g2[0]

    spread(lambda h: None)
    swap.wait_send()
    for q in range(1, NZ):
        init_z(q).wait_send()

    first = img[...]
    d[...] = first
    r[...] = first
    rr[...] = jnp.broadcast_to(total(first * first), (8, 128))
    x[...] = jnp.zeros((8, 128), F32)

    def set_trial():
        high, low = split(d[...])
        d2[0:128, :] = high
        d2[128:256, :] = low

    def inter(n, count):
        eye = lax.broadcasted_iota(jnp.int32, (128, 128), 0) == lax.broadcasted_iota(jnp.int32, (128, 128), 1)
        contract = (((1,), (1,)), ((), ()))
        size = count * O
        at = pl.ds(pl.multiple_of(n * size, size), size)
        both = lax.dot_general(bhi[at, :], d2[...], contract, preferred_element_type=F32)
        rest = lax.dot_general(blo[at, :], d2[0:128, :], contract, preferred_element_type=F32)
        y = both[:, 0:128] + both[:, 128:256] + rest
        for i in range(count):
            block = y[i * 128:(i + 1) * 128, :]
            coulomb = total(jnp.where(eye, block, 0.0))
            zh, zl = split(jnp.where(eye, 4.0 * coulomb, 0.0) - block)
            cols = pl.ds(pl.multiple_of(n * size + i * 128, 128), 128)
            zs[0:128, cols] = zh
            zs[128:256, cols] = zl

    def outer(h):
        def body(n, carry):
            cols = pl.ds(pl.multiple_of(h * HALF + n * HALF, 256), HALF)
            to = pl.ds(pl.multiple_of(h * HALF + n * HALF, 256), HALF)
            both = jnp.dot(zs[...], bhi[:, cols], preferred_element_type=F32)
            rest = jnp.dot(zs[0:128, :], blo[:, cols], preferred_element_type=F32)
            part[:, to] = both[0:128] + both[128:256] + rest
            return carry

        body(0, 0)

    set_trial()
    local.wait()

    def arrive(n, carry):
        for q in ISSUE:
            exchange(q, n).wait_send()

            @pl.when(n + AHEAD < CHUNKS)
            def _():
                exchange(q, n + AHEAD).start()

        for q in ISSUE:
            exchange(q, n).wait_recv()

        def body(i, carry):
            p = n * NC + i
            at = pl.ds(pl.multiple_of(p * 128, 128), 128)
            for q in range(NZ):
                high, low = split(recv[q, p])
                bhi[at, q * 128:(q + 1) * 128] = high
                blo[at, q * 128:(q + 1) * 128] = low
            return carry

        lax.fori_loop(0, NC, body, 0)
        inter(n, NC)
        return carry

    lax.fori_loop(0, CHUNKS, arrive, 0)

    def span(h, scalar):
        return slice(h * HALF, W if h == 1 and scalar else (h + 1) * HALF)

    def reduce(before, collect, scalar):
        def pair(h):
            cols = span(h, scalar)
            theirs = rows(part, 8 * (1 - c), 64).at[:, cols]
            return remote(theirs, cbuf.at[:, cols], rsc_s.at[h], rsc_r.at[h], partner)

        def to_chip(t, h):
            chip = 8 * c + t
            j = lax.rem(chip - m + NM, NM)
            cols = span(h, scalar)
            return remote(
                rows(part, chip).at[:, cols], xbuf.at[j, :, cols], rsx_s.at[h, t], rsx_r.at[h, j], at_m(chip)
            )

        for h in range(2):
            outer(h)
            if h == 1:
                before()
            pair(h).start()
        for h in range(2):
            pair(h).wait_recv()
            cols = span(h, scalar)
            half = rows(part, 8 * c, 64)
            half[:, cols] = half[:, cols] + cbuf[:, cols]
            for t in range(8):
                @pl.when(8 * c + t != m)
                def _():
                    to_chip(t, h).start()

        @pl.when(owner)
        def _():
            for h in range(2):
                cols = span(h, scalar)
                acc = rows(part, m)[:, cols]
                for j in range(1, NM):
                    slot = xbuf.at[j, :, cols]
                    remote(slot, slot, rsx_s.at[0, 0], rsx_r.at[h, j], partner).wait_recv()
                    acc = acc + xbuf[j, :, cols]
                collect(h, acc)

        def finish():
            for h in range(2):
                for t in range(8):
                    @pl.when(8 * c + t != m)
                    def _():
                        to_chip(t, h).wait_send()
                pair(h).wait_send()

        return finish

    def iterate(step, carry):
        slot = lax.rem(step, 2)

        def to_z(q, h):
            block = zbuf.at[slot, z, :, h * HALF:(h + 1) * HALF]
            return remote(block, block, zz_s.at[slot, h, q], zz_r.at[slot, h, q], at_z(SHIFT[q]))

        def collect(h, acc):
            zbuf[slot, z, :, h * HALF:(h + 1) * HALF] = acc
            for q in ISSUE:
                to_z(q, h).start()

        def ready(h):
            cols = slice(h * HALF, (h + 1) * HALF)
            for q in range(1, NZ):
                to_z(q, h).wait_recv()
            acc = gap[:, cols] * rows(d, m)[:, cols]
            for s in range(NZ):
                acc = acc + zbuf[slot, s, :, cols]
            rows(img, m)[:, cols] = acc

        finish = reduce(lambda: None, collect, False)
        spread(ready)
        finish()

        @pl.when(owner)
        def _():
            for h in range(2):
                for q in range(1, NZ):
                    to_z(q, h).wait_send()

        image, trial = img[...], d[...]
        old = rr[0:1, 0:1]
        alpha = old / total(trial * image)
        x[...] = x[...] + alpha * rows(d, m)[:, here]
        left = r[...] - alpha * image
        new = total(left * left)
        r[...] = left
        d[...] = left + (new / old) * trial
        rr[...] = jnp.broadcast_to(new, (8, 128))
        set_trial()
        inter(0, NP)
        return carry

    lax.fori_loop(0, ITERS - 1, iterate, 0)

    own_d = rows(d, m)[:, here]

    def add_curvature():
        own_gap = total(gap[:, here] * own_d * own_d)
        curve = total(d[...] * part[:, 0:V]) + jnp.where(owner, own_gap, jnp.zeros_like(own_gap))
        part[:, V:W] = jnp.broadcast_to(curve, (128, 128))

    def to_peers(q, core):
        to = lax.rem(z + SHIFT[q] + NZ, NZ)
        dev = (2 * m + lax.rem(c + core, 2), to)
        return (
            remote(zsend.at[NZ], sbuf.at[q], sc_s.at[core, q], sc_r.at[q], dev),
            remote(zsend.at[to], tbuf.at[q], rsz_s.at[core, q], rsz_r.at[q], dev),
        )

    sends = [(0, 1)] + [(q, core) for q in ISSUE for core in range(2)]

    def last(h, acc):
        for s in range(4):
            zsend[4 * h + s] = acc[:, s * 128:(s + 1) * 128]
        if h == 0:
            return
        zsend[NZ] = acc[:, HALF:HALF + 128]
        for q, core in sends[1:] + sends[:1]:
            for copy in to_peers(q, core):
                copy.start()
        tbuf[0] = zsend[z]
        sbuf[0] = zsend[NZ]

    finish = reduce(add_curvature, last, True)

    @pl.when(jnp.logical_not(owner))
    def _():
        for copy in to_peers(0, 1):
            copy.wait_recv()

    tile = gap[:, here] * own_d + tbuf[0]
    curve = sbuf[0]
    for q in range(1, NZ):
        for copy in to_peers(q, 0):
            copy.wait_recv()
        tile = tile + tbuf[q]
        curve = curve + sbuf[q]

    alpha = rr[...] / curve
    answer = x[...] + alpha * own_d
    left = rows(r, m)[:, here] - alpha * tile
    lower = c == 0
    out[0] = jnp.where(lower, answer[0:4], answer[4:8])
    out[1] = jnp.where(lower, left[0:4], left[4:8])

    finish()

    @pl.when(owner)
    def _():
        for q, core in sends:
            for copy in to_peers(q, core):
                copy.wait_send()


def on_device(integrals, occupied_energy, virtual_energy, right_side):
    dma = pltpu.SemaphoreType.DMA
    vmem = pl.BlockSpec(memory_space=pltpu.VMEM)
    result = pl.pallas_call(
        kernel,
        out_shape=jax.ShapeDtypeStruct((2, 4, 128), F32),
        in_specs=[pl.BlockSpec(memory_space=pl.ANY)] * 4,
        out_specs=vmem,
        scratch_shapes=[
            pltpu.SMEM((4,), F32),
            pltpu.VMEM((1, 128), F32),
            pltpu.VMEM((4, 128), F32),
            pltpu.VMEM((NZ, NP, 128, 128), F32),
            pltpu.VMEM((NP * O, V), BF16),
            pltpu.VMEM((NP * O, V), BF16),
            pltpu.VMEM((O, V), F32),
            pltpu.VMEM((O, V), F32),
            pltpu.VMEM((O, V), F32),
            pltpu.VMEM((O, W), F32),
            pltpu.VMEM((64, W), F32),
            pltpu.VMEM((NM, 8, W), F32),
            pltpu.VMEM((2, NZ, 8, V), F32),
            pltpu.VMEM((NZ + 1, 8, 128), F32),
            pltpu.VMEM((NZ, 8, 128), F32),
            pltpu.VMEM((NZ, 8, 128), F32),
            pltpu.VMEM((2, 8, V), F32),
            pltpu.VMEM((2, 8, V), F32),
            pltpu.VMEM((8, V), F32),
            pltpu.VMEM((8, 128), F32),
            pltpu.VMEM((256, V), BF16),
            pltpu.VMEM((256, NP * O), BF16),
            pltpu.VMEM((8, 128), F32),
            dma((NZ, CHUNKS)), dma((NZ, CHUNKS)), dma((4,)),
            dma((NZ,)), dma((NZ,)), dma((2,)), dma((2, NM)), dma((2, 8)), dma((2, 8)), dma((2, 8)),
            dma((2,)), dma((2,)), dma((2, 8)), dma((2, NM)), dma((2, 2, NZ)), dma((2, 2, NZ)),
            dma((2, NZ)), dma((NZ,)), dma((2, NZ)), dma((NZ,)),
        ],
        compiler_params=pltpu.CompilerParams(
            collective_id=0, has_side_effects=True, vmem_limit_bytes=60 << 20
        ),
        name="solve",
    )(integrals, occupied_energy, virtual_energy.reshape(1, 128), right_side.T)
    return result[0].T, result[1].T


def solution(mesh):
    in_specs = (P("aux", None, "vir"), P("aux"), P("vir"), P("vir", "aux"))
    out_specs = (P("vir", "aux"), P("vir", "aux"))
    return jax.shard_map(
        on_device, mesh=mesh, in_specs=in_specs, out_specs=out_specs, check_vma=False
    )
```
